32 devices in a mesh: pty: 16 (over z, y, core), tx: 2 (over x).
Axes of the slice: x: 2, y: 2, z: 4, core: 2. Of those that a mesh axis runs over, the one named last changes fastest.
Arguments:
- state: float32 [5, 384, 64, 128], P(None, 'pty', 'tx'), may hold values from -6 to 6
- sound_speed_sq: float32 [384, 64, 128], P('pty', 'tx'), may hold values from 0.05 to 0.3
- buoyancy_freq_sq: float32 [128], replicated, may hold values from 0.2 to 2
- adjacency: int32 [6, 4, 3], replicated, may hold values from 0 to 5, as said below
Outputs:
- advanced: float32 [5, 384, 64, 128], P(None, 'pty', 'tx')
The draws below stay inside these ranges and needn't reach their ends.
Inputs may be any that keep to these rules, and one draw needn't show every extreme that they name: adjacency[k, e] = (q, f, r): edge e of panel k touches edge f of panel q, position s meeting position s of f if r = 0 and 63 - s if r = 1; the relation is symmetric, q differs from k, and the six panels with their edges close into a cube.
All inputs are finite; a program needn't handle non-finite values.
Results may differ from the reference program's by a relative error of at most 0.00002.
Values sent between devices are 32-bit elements; how exact they have to be, the bound alone decides.
A program may use at most 64 MiB of HBM per device.

```python
import math
import jax
import jax.numpy as jnp
from jax import lax

LEV = 128
PANEL = 64
ROWS = 384
SHIFT = 12


def cross_three(first, second):
    return [first[1] * second[2] - first[2] * second[1], first[2] * second[0] - first[0] * second[2], first[0] * second[1] - first[1] * second[0]]


def same_three(first, second):
    return first[0] == second[0] and first[1] == second[1] and (first[2] == second[2])


def cube_table():
    normals = [[1, 0, 0], [-1, 0, 0], [0, 1, 0], [0, -1, 0], [0, 0, 1], [0, 0, -1]]
    middles = []
    for normal in normals:
        axis_i = [0, 1, 0] if normal[0] != 0 else [1, 0, 0]
        axis_j = cross_three(normal, axis_i)
        middles.append([[normal[0] - axis_i[0], normal[1] - axis_i[1], normal[2] - axis_i[2]], [normal[0] + axis_j[0], normal[1] + axis_j[1], normal[2] + axis_j[2]], [normal[0] + axis_i[0], normal[1] + axis_i[1], normal[2] + axis_i[2]], [normal[0] - axis_j[0], normal[1] - axis_j[1], normal[2] - axis_j[2]]])
    result = [[[0, 0] for edge_index in range(4)] for face_index in range(6)]
    for face_index in range(6):
        for edge_index in range(4):
            for other_face in range(6):
                for other_edge in range(4):
                    if other_face != face_index and same_three(middles[face_index][edge_index], middles[other_face][other_edge]):
                        result[face_index][edge_index] = [other_face, other_edge]
    return result


def draw_adjacency(key, part):
    canon = jnp.asarray(cube_table(), dtype=jnp.int32)
    key_perm, key_turn = jax.random.split(jax.random.fold_in(key, 17))
    labels = jax.random.permutation(key_perm, 6).astype(jnp.int32)
    turns = jax.random.randint(key_turn, (6,), 0, 4, dtype=jnp.int32)
    face_ids = jnp.arange(6, dtype=jnp.int32)[:, None]
    local_edge = jnp.arange(4, dtype=jnp.int32)[None, :]
    canon_edge = (local_edge + turns[:, None]) % 4
    other_face = canon[face_ids, canon_edge, 0]
    other_canon = canon[face_ids, canon_edge, 1]
    other_local = (other_canon - turns[other_face]) % 4
    flag = ((local_edge < 2) == (other_local < 2)).astype(jnp.int32)
    by_face = jnp.stack([labels[other_face], other_local.astype(jnp.int32), flag], axis=-1)
    return jnp.zeros((6, 4, 3), jnp.int32).at[labels].set(by_face)


def level_of(own_key, shape, cuts, smallest, high):
    def one(dim, blocks):
        steps = jax.random.uniform(jax.random.fold_in(jax.random.fold_in(own_key, 6), dim), (blocks,), jnp.float32, smallest / len(cuts), high / len(cuts))
        return jnp.repeat(jnp.exp(steps), shape[dim] // blocks).reshape((-1,) + (1,) * (len(shape) - dim - 1))

    gain = one(*cuts[0])
    for cut in cuts[1:]:
        gain = gain * one(*cut)
    return gain


def gaussian(own_key, dims, deviation, limit, shards=(), kind=jnp.bfloat16):
    values = jax.random.normal(own_key, dims, jnp.float32) * deviation
    if len(shards) > 0:
        values = level_of(own_key, dims, shards, -0.22, 0.18) * values
    return jnp.clip(values, min=-limit, max=limit).astype(kind)


def setup_inputs(seed: int = 0) -> dict:
    key_list = jax.random.split(jax.random.key(seed), 5)
    return {
        "state": gaussian(key_list[0], (5, ROWS, PANEL, LEV), 1.0, 6.0, ((1, 16), (2, 2)), jnp.float32),
        "sound_speed_sq": jnp.clip(jnp.exp(math.log(0.3) - 1.7917595 * jax.random.uniform(key_list[1], (ROWS, PANEL, LEV), jnp.float32) ** level_of(key_list[1], (ROWS, PANEL, LEV), ((0, 16), (1, 2)), -0.2, 0.2)), 0.05, 0.3),
        "buoyancy_freq_sq": jnp.clip(jnp.exp(jax.random.uniform(key_list[2], (LEV,), jnp.float32, math.log(0.2), math.log(2.0))), 0.2, 2.0),
        "adjacency": draw_adjacency(jax.random.fold_in(key_list[4], 71), 0),
    }


STEP = 0.5


def along_axis(values, axis):
    length = values.shape[axis]
    lowest = lax.slice_in_dim(values, 1, 2, axis=axis) - lax.slice_in_dim(values, 0, 1, axis=axis)
    middle = 0.5 * (lax.slice_in_dim(values, 2, length, axis=axis) - lax.slice_in_dim(values, 0, length - 2, axis=axis))
    highest = lax.slice_in_dim(values, length - 1, length, axis=axis) - lax.slice_in_dim(values, length - 2, length - 1, axis=axis)
    return jnp.concatenate([lowest, middle, highest], axis=axis)


def wall_diff(values):
    lowest = values[..., 1:2] + values[..., 0:1]
    middle = 0.5 * (values[..., 2:] - values[..., :-2])
    highest = -(values[..., -1:] + values[..., -2:-1])
    return jnp.concatenate([lowest, middle, highest], axis=-1)


def panel_rate(fields, speed_sq, freq_sq, sat_p, sat_n):
    vel_u, vel_v, vel_w, pressure, buoyancy = fields[0], fields[1], fields[2], fields[3], fields[4]
    tend_u = -along_axis(pressure, 0)
    tend_v = -along_axis(pressure, 1)
    tend_w = -along_axis(pressure, 2) + buoyancy
    tend_b = -freq_sq * vel_w
    tend_p = -speed_sq * (along_axis(vel_u, 0) + along_axis(vel_v, 1) + wall_diff(vel_w))
    tend_p = tend_p.at[0].add(speed_sq[0] * sat_p[0])
    tend_u = tend_u.at[0].add(-sat_n[0])
    tend_p = tend_p.at[:, -1].add(speed_sq[:, -1] * sat_p[1])
    tend_v = tend_v.at[:, -1].add(sat_n[1])
    tend_p = tend_p.at[-1].add(speed_sq[-1] * sat_p[2])
    tend_u = tend_u.at[-1].add(sat_n[2])
    tend_p = tend_p.at[:, 0].add(speed_sq[:, 0] * sat_p[3])
    tend_v = tend_v.at[:, 0].add(-sat_n[3])
    return jnp.stack([tend_u, tend_v, tend_w, tend_p, tend_b])


def section_edges(current, adjacency):
    vel_u, vel_v, pressure = current[0], current[1], current[3]
    edge_p = jnp.stack([pressure[:, 0], pressure[:, :, -1], pressure[:, -1], pressure[:, :, 0]], axis=1)
    edge_n = jnp.stack([-vel_u[:, 0], vel_v[:, :, -1], vel_u[:, -1], -vel_v[:, :, 0]], axis=1)
    other_panel = adjacency[:, :, 0]
    other_edge = adjacency[:, :, 1]
    flipped = adjacency[:, :, 2] == 1
    near_p = edge_p[other_panel, other_edge]
    near_n = edge_n[other_panel, other_edge]
    near_p = jnp.where(flipped[:, :, None, None], near_p[:, :, ::-1], near_p)
    near_n = jnp.where(flipped[:, :, None, None], near_n[:, :, ::-1], near_n)
    return edge_n + near_n, edge_p - near_p


def advance(base, current, speed_panels, freq_sq, adjacency, weight_base, weight_new):
    sat_p, sat_n = section_edges(current, adjacency)

    def one_panel(index):
        fields = lax.dynamic_index_in_dim(current, index, 1, keepdims=False)
        base_panel = lax.dynamic_index_in_dim(base, index, 1, keepdims=False)
        speed_sq = lax.dynamic_index_in_dim(speed_panels, index, 0, keepdims=False)
        panel_sat_p = lax.dynamic_index_in_dim(sat_p, index, 0, keepdims=False)
        panel_sat_n = lax.dynamic_index_in_dim(sat_n, index, 0, keepdims=False)
        rate = panel_rate(fields, speed_sq, freq_sq, panel_sat_p, panel_sat_n)
        return weight_base * base_panel + weight_new * (fields + STEP * rate)

    return jnp.moveaxis(lax.map(one_panel, jnp.arange(6, dtype=jnp.int32)), 0, 1)


def reference(state, sound_speed_sq, buoyancy_freq_sq, adjacency):
    base = jnp.roll(state, -SHIFT, axis=1).reshape(5, 6, PANEL, PANEL, LEV)
    speed_panels = jnp.roll(sound_speed_sq, -SHIFT, axis=0).reshape(6, PANEL, PANEL, LEV)
    section_one = advance(base, base, speed_panels, buoyancy_freq_sq, adjacency, 0.0, 1.0)
    section_two = advance(base, section_one, speed_panels, buoyancy_freq_sq, adjacency, 0.75, 0.25)
    result = advance(base, section_two, speed_panels, buoyancy_freq_sq, adjacency, 1.0 / 3.0, 2.0 / 3.0)
    return jnp.roll(result.reshape(5, ROWS, PANEL, LEV), SHIFT, axis=1)
```

```python
import functools

import jax
import jax.numpy as jnp
from jax import lax
from jax.experimental import pallas as pl
from jax.experimental.pallas import tpu as pltpu
from jax.sharding import PartitionSpec as P

STEP = 0.5
MESH = pl.DeviceIdType.MESH
ORDER = (0, 3, 1, 2, 4)
U, PR, V, W, B = range(5)
(SEND_UP, RECV_UP, SEND_DN, RECV_DN, SEND_L, RECV_L, SEND_R, RECV_R, ONE_C, ONE_C2, ONE_R,
 ONE_R2, TABLE, TWO, BACK_C, BACK_R, LOAD) = range(17)


def divide(x, d, limit):
    if d & (d - 1) == 0:
        return x >> (d.bit_length() - 1)
    factor = (1 << 16) // d + 1
    assert all((i * factor) >> 16 == i // d for i in range(limit)) and limit * factor < 2**31
    return (x * factor) >> 16


def kernel(n, t_count, rows, cols, levels, state, speed, freq, adj, out, buf, col, row, halo,
           tab, pick, back_c, back_r, junk, junk2, speed_v, work, sems):
    panel = cols * t_count
    total = 6 * panel
    shift = rows // 2
    row_blocks, col_blocks = rows // 4, cols // 4
    blocks = panel // 4
    groups = blocks // 2
    pairs = n // 4
    stride = max(1, t_count // -(-groups // pairs))
    edges = [(k * panel + shift) // rows for k in range(6)]
    places = [(k * panel + shift) % rows for k in range(6)]
    mask = sum(1 << m for m in range(n // 2) if 2 * m in edges)

    pty = lax.axis_index("pty")
    tx = lax.axis_index("tx")
    up = jnp.where(pty == 0, n - 1, pty - 1)
    down = jnp.where(pty == n - 1, 0, pty + 1)
    at_west = tx == 0
    at_east = tx == t_count - 1
    on_edge = at_west | at_east

    first_row = jnp.int32(-1)
    start_panel = jnp.int32(0)
    for k in range(6):
        first_row = jnp.where(pty == edges[k], places[k], first_row)
        start_panel = jnp.where(pty == edges[k], k, start_panel)
    end_panel = jnp.where(start_panel == 0, 5, start_panel - 1)
    has_start = first_row >= 0

    def holder(half, group):
        pair = group % pairs if pairs & (pairs - 1) else group & (pairs - 1)
        place = half * pairs + pair
        return (2 * place + ((mask >> place) & 1), divide(group, pairs, 4096) * stride)

    my_place = pty >> 1
    my_half = divide(my_place, pairs, 4096)
    my_pair = my_place - my_half * pairs
    my_group = divide(tx, stride, 4096) * pairs + my_pair
    is_holder = (
        ((pty & 1) == ((mask >> my_place) & 1))
        & (tx == divide(tx, stride, 4096) * stride)
        & (my_group < groups)
    )

    def push(src, dst, spare, send, recv, there):
        same = (there[0] == pty) & (there[1] == tx)

        @pl.when(same)
        def _():
            pltpu.make_async_copy(src, dst, recv).start()
            pltpu.make_async_copy(src, spare, send).start()

        @pl.when(jnp.logical_not(same))
        def _():
            pltpu.make_async_remote_copy(
                src_ref=src, dst_ref=dst, send_sem=send, recv_sem=recv,
                device_id=there, device_id_type=MESH,
            ).start()

    def done(ref, sem):
        pltpu.make_async_copy(ref, ref, sem).wait()

    loads = [
        pltpu.make_async_copy(state.at[ORDER[f]], buf.at[0, f, pl.ds(1, rows)], sems.at[LOAD, 0])
        for f in range(5)
    ]
    for copy in loads:
        copy.start()
    load_speed = pltpu.make_async_copy(speed, speed_v, sems.at[LOAD, 1])
    load_speed.start()
    done(buf.at[0, :, pl.ds(1, rows)], sems.at[LOAD, 0])

    lane = lax.broadcasted_iota(jnp.int32, (cols, levels), 1)
    line = lax.broadcasted_iota(jnp.int32, (cols, levels), 0)
    low, high = lane == 0, lane == levels - 1
    lev_half = jnp.where(low | high, 1.0, 0.5).astype(jnp.float32)
    west_line, east_line = line == 0, line == cols - 1
    col_half = jnp.where((west_line & at_west) | (east_line & at_east), 1.0, 0.5).astype(jnp.float32)
    sub = lax.broadcasted_iota(jnp.int32, (8, levels), 0)
    west_sign = jnp.where(at_west, -1.0, 1.0).astype(jnp.float32)

    def row_sends(s, there, src_row, dst_row, send, recv):
        return pltpu.make_async_remote_copy(
            src_ref=buf.at[s, pl.ds(0, 2), src_row], dst_ref=buf.at[s, pl.ds(0, 2), dst_row],
            send_sem=sems.at[send, s], recv_sem=sems.at[recv, s],
            device_id=(there, tx), device_id_type=MESH,
        )

    def col_sends(s, there, side, send, recv):
        return pltpu.make_async_remote_copy(
            src_ref=col.at[s, side], dst_ref=halo.at[s, 1 - side],
            send_sem=sems.at[send, s], recv_sem=sems.at[recv, s],
            device_id=(pty, there), device_id_type=MESH,
        )

    def stage(s, carry):
        weight_base = jnp.where(s == 0, 0.0, jnp.where(s == 1, 0.75, 1.0 / 3.0)).astype(jnp.float32)
        weight_new = jnp.where(s == 0, 1.0, jnp.where(s == 1, 0.25, 2.0 / 3.0)).astype(jnp.float32)
        weight_rate = weight_new * STEP

        def pack_col(ib, carry):
            for side in range(2):
                j = 0 if side == 0 else cols - 1
                for t in range(4):
                    i = 1 + 4 * ib + t
                    p = buf[s, PR, i, j : j + 1]
                    v = buf[s, V, i, j : j + 1]
                    col[s, side, ib, t : t + 1] = p
                    col[s, side, ib, 4 + t : 5 + t] = v * west_sign if side == 0 else v
            return carry

        lax.fori_loop(0, row_blocks, pack_col, 0)

        @pl.when(has_start)
        def _():
            for e in range(2):
                i = first_row + 1 - e
                for m in range(col_blocks // 2):
                    p = buf[s, PR, i, 8 * m : 8 * m + 8]
                    u = buf[s, U, i, 8 * m : 8 * m + 8]
                    if e == 0:
                        u = -u
                    row[s, e * col_blocks + 2 * m] = jnp.where(sub < 4, p, pltpu.roll(u, 4, 0))
                    row[s, e * col_blocks + 2 * m + 1] = jnp.where(sub < 4, pltpu.roll(p, 4, 0), u)

        @pl.when(on_edge)
        def _():
            side = jnp.where(at_west, 0, 1)
            edge = jnp.where(at_west, 3, 1)

            def one(ib, carry):
                place = pty * rows + 4 * ib - shift
                place = jnp.where(place < 0, place + total, place)
                k = divide(place, panel, total)
                b = (place - k * panel) >> 2
                far = b >= groups
                slot = (k * 4 + edge) * 2 + jnp.where(far, 1, 0)
                group = jnp.where(far, blocks - 1 - b, b)
                for half in range(2):
                    push(col.at[s, side, ib], tab.at[s, slot], junk.at[s, half, ib],
                         sems.at[ONE_C + half, s], sems.at[TABLE, s], holder(half, group))
                return carry

            lax.fori_loop(0, row_blocks, one, 0)

        @pl.when(has_start)
        def _():
            def one(m, carry):
                b = tx * col_blocks + m
                far = b >= groups
                group = jnp.where(far, blocks - 1 - b, b)
                for e in range(2):
                    k = start_panel if e == 0 else end_panel
                    slot = (k * 4 + 2 * e) * 2 + jnp.where(far, 1, 0)
                    for half in range(2):
                        push(row.at[s, e * col_blocks + m], tab.at[s, slot],
                             junk.at[s, half, row_blocks + e * col_blocks + m],
                             sems.at[ONE_R + half, s], sems.at[TABLE, s], holder(half, group))
                return carry

            lax.fori_loop(0, col_blocks, one, 0)

        row_sends(s, up, 1, rows + 1, SEND_UP, RECV_UP).start()
        row_sends(s, down, rows, 0, SEND_DN, RECV_DN).start()

        @pl.when(tx > 0)
        def _():
            col_sends(s, tx - 1, 0, SEND_L, RECV_L).start()

        @pl.when(tx < t_count - 1)
        def _():
            col_sends(s, tx + 1, 1, SEND_R, RECV_R).start()

        def vertical(ib, carry):
            rate = weight_rate * freq[0:1]
            for t in range(4):
                i = 1 + 4 * ib + t
                p, w, b = buf[s, PR, i], buf[s, W, i], buf[s, B, i]
                above = jnp.where(high, p, pltpu.roll(p, levels - 1, 1))
                below = jnp.where(low, p, pltpu.roll(p, 1, 1))
                diff = lev_half * (above - below)
                buf[s + 1, W, i] = weight_base * buf[0, W, i] + (weight_new * w + weight_rate * (b - diff))
                buf[s + 1, B, i] = weight_base * buf[0, B, i] + (weight_new * b - rate * w)
            return carry

        lax.fori_loop(0, row_blocks, vertical, 0)

        @pl.when(is_holder)
        def _():
            done(tab.at[s], sems.at[TABLE, s])
            work[...] = tab[s]

            def one(kk, carry):
                k = my_half * 3 + kk
                for e in range(4):
                    entry = (k * 4 + e) * 3
                    partner = (adj[entry] * 4 + adj[entry + 1]) * 2
                    flip = adj[entry + 2]
                    for far in range(2):
                        b = my_group if far == 0 else blocks - 1 - my_group
                        value = work[partner + (flip if far == 0 else 1 - flip)]
                        two = jnp.where((sub & 2) == 0, pltpu.roll(value, 6, 0), pltpu.roll(value, 2, 0))
                        turned = jnp.where((sub & 1) == 0, pltpu.roll(two, 7, 0), pltpu.roll(two, 1, 0))
                        slot = kk * 8 + e * 2 + far
                        pick[s, slot] = jnp.where(flip == 1, turned, value)
                        if e == 1 or e == 3:
                            place = k * panel + 4 * b + shift
                            place = jnp.where(place >= total, place - total, place)
                            owner = divide(place, rows, total)
                            index = (place - owner * rows) >> 2
                            push(pick.at[s, slot], back_c.at[s, index], junk2.at[s, slot],
                                 sems.at[TWO, s], sems.at[BACK_C, s],
                                 (owner, t_count - 1 if e == 1 else 0))
                        else:
                            place = k * panel + shift + (0 if e == 0 else panel - 1)
                            place = jnp.where(place >= total, place - total, place)
                            owner = divide(place, rows, total)
                            owner_tx = divide(b, col_blocks, total)
                            index = (e // 2) * col_blocks + b - owner_tx * col_blocks
                            push(pick.at[s, slot], back_r.at[s, index], junk2.at[s, slot],
                                 sems.at[TWO, s], sems.at[BACK_R, s], (owner, owner_tx))
                return carry

            lax.fori_loop(0, 3, one, 0)

        row_sends(s, up, 1, rows + 1, SEND_UP, RECV_UP).wait_recv()
        row_sends(s, down, rows, 0, SEND_DN, RECV_DN).wait_recv()

        @pl.when(tx > 0)
        def _():
            done(halo.at[s, 0], sems.at[RECV_R, s])

        @pl.when(tx < t_count - 1)
        def _():
            done(halo.at[s, 1], sems.at[RECV_L, s])

        @pl.when(s == 0)
        def _():
            load_speed.wait()

        def horizontal(ib, carry):
            for t in range(4):
                i = 1 + 4 * ib + t
                is_start, is_end = i - 1 == first_row, i == first_row
                row_half = jnp.where(is_start | is_end, 1.0, 0.5).astype(jnp.float32)
                u, p, v, w = buf[s, U, i], buf[s, PR, i], buf[s, V, i], buf[s, W, i]

                def along_rows(f, here):
                    after = jnp.where(is_end, here, buf[s, f, i + 1])
                    before = jnp.where(is_start, here, buf[s, f, i - 1])
                    return row_half * (after - before)

                def along_cols(here, offset):
                    left = halo[s, 0, ib, offset + t : offset + t + 1]
                    right = halo[s, 1, ib, offset + t : offset + t + 1]
                    left = jnp.where(at_west, here[0:1], left)
                    right = jnp.where(at_east, here[cols - 1 :], right)
                    after = jnp.where(east_line, right, pltpu.roll(here, cols - 1, 0))
                    before = jnp.where(west_line, left, pltpu.roll(here, 1, 0))
                    return col_half * (after - before)

                above = jnp.where(high, -w, pltpu.roll(w, levels - 1, 1))
                below = jnp.where(low, -w, pltpu.roll(w, 1, 1))
                wall = lev_half * (above - below)
                buf[s + 1, U, i] = weight_base * buf[0, U, i] + (
                    weight_new * u - weight_rate * along_rows(PR, p))
                buf[s + 1, V, i] = weight_base * buf[0, V, i] + (
                    weight_new * v - weight_rate * along_cols(p, 0))
                buf[s + 1, PR, i] = weight_base * buf[0, PR, i] + (
                    weight_new * p - (weight_rate * speed_v[i - 1]) * (
                        along_rows(U, u) + along_cols(v, 4) + wall))
            return carry

        lax.fori_loop(0, row_blocks, horizontal, 0)

        @pl.when(has_start)
        def _():
            done(back_r.at[s], sems.at[BACK_R, s])
            for e in range(2):
                i = first_row + 1 - e
                sign = -1.0 if e == 0 else 1.0
                for m in range(col_blocks // 2):
                    one, two = back_r[s, e * col_blocks + 2 * m], back_r[s, e * col_blocks + 2 * m + 1]
                    p_there = jnp.where(sub < 4, one, pltpu.roll(two, 4, 0))
                    n_there = jnp.where(sub < 4, pltpu.roll(one, 4, 0), two)
                    at = pl.ds(8 * m, 8)
                    n_here = sign * buf[s, U, i, at]
                    buf[s + 1, PR, i, at] += weight_rate * speed_v[i - 1, at] * (n_here + n_there)
                    buf[s + 1, U, i, at] += (sign * weight_rate) * (buf[s, PR, i, at] - p_there)

        for side in range(2):
            @pl.when(at_west if side == 0 else at_east)
            def _():
                done(back_c.at[s], sems.at[BACK_C, s])
                sign = -1.0 if side == 0 else 1.0
                j = 0 if side == 0 else cols - 1

                def one(ib, carry):
                    for t in range(4):
                        i = 1 + 4 * ib + t
                        p_here = col[s, side, ib, t : t + 1]
                        n_here = col[s, side, ib, 4 + t : 5 + t]
                        p_there = back_c[s, ib, t : t + 1]
                        n_there = back_c[s, ib, 4 + t : 5 + t]
                        buf[s + 1, PR, i, j : j + 1] += (
                            weight_rate * speed_v[i - 1, j : j + 1] * (n_here + n_there))
                        buf[s + 1, V, i, j : j + 1] += (sign * weight_rate) * (p_here - p_there)
                    return carry

                lax.fori_loop(0, row_blocks, one, 0)

        return carry

    @pl.when(at_west)
    def _():
        halo[:, 0] = jnp.zeros((3, row_blocks, 8, levels), jnp.float32)

    @pl.when(at_east)
    def _():
        halo[:, 1] = jnp.zeros((3, row_blocks, 8, levels), jnp.float32)

    lax.fori_loop(0, 3, stage, 0)

    stores = [
        pltpu.make_async_copy(buf.at[3, f, pl.ds(1, rows)], out.at[ORDER[f]], sems.at[LOAD, 2])
        for f in range(5)
    ]
    for copy in stores:
        copy.start()

    def finish(s, carry):
        row_sends(s, up, 1, rows + 1, SEND_UP, RECV_UP).wait_send()
        row_sends(s, down, rows, 0, SEND_DN, RECV_DN).wait_send()

        @pl.when(tx > 0)
        def _():
            done(col.at[s, 0], sems.at[SEND_L, s])

        @pl.when(tx < t_count - 1)
        def _():
            done(col.at[s, 1], sems.at[SEND_R, s])

        for half in range(2):
            @pl.when(on_edge)
            def _():
                done(col.at[s, 0], sems.at[ONE_C + half, s])

            @pl.when(has_start)
            def _():
                done(row.at[s], sems.at[ONE_R + half, s])

        @pl.when(is_holder)
        def _():
            done(pick.at[s], sems.at[TWO, s])

        return carry

    lax.fori_loop(0, 3, finish, 0)
    done(buf.at[3, :, pl.ds(1, rows)], sems.at[LOAD, 2])


def on_device(n, t_count, state, speed, freq, adjacency):
    _, rows, cols, levels = state.shape
    rb, cb = rows // 4, cols // 4
    f32 = jnp.float32
    return pl.pallas_call(
        functools.partial(kernel, n, t_count, rows, cols, levels),
        out_shape=jax.ShapeDtypeStruct(state.shape, f32),
        in_specs=[
            pl.BlockSpec(memory_space=pl.ANY),
            pl.BlockSpec(memory_space=pl.ANY),
            pl.BlockSpec(memory_space=pltpu.VMEM),
            pl.BlockSpec(memory_space=pltpu.SMEM),
        ],
        out_specs=pl.BlockSpec(memory_space=pl.ANY),
        scratch_shapes=[
            pltpu.VMEM((4, 5, rows + 2, cols, levels), f32),
            pltpu.VMEM((3, 2, rb, 8, levels), f32),
            pltpu.VMEM((3, 2 * cb, 8, levels), f32),
            pltpu.VMEM((3, 2, rb, 8, levels), f32),
            pltpu.VMEM((3, 48, 8, levels), f32),
            pltpu.VMEM((3, 24, 8, levels), f32),
            pltpu.VMEM((3, rb, 8, levels), f32),
            pltpu.VMEM((3, 2 * cb, 8, levels), f32),
            pltpu.VMEM((3, 2, rb + 2 * cb, 8, levels), f32),
            pltpu.VMEM((3, 24, 8, levels), f32),
            pltpu.VMEM((rows, cols, levels), f32),
            pltpu.VMEM((48, 8, levels), f32),
            pltpu.SemaphoreType.DMA((17, 3)),
        ],
        compiler_params=pltpu.CompilerParams(
            has_side_effects=True, vmem_limit_bytes=32 * 1024 * 1024
        ),
    )(state, speed, freq.reshape(1, levels), adjacency.reshape(-1))


def solution(mesh):
    in_specs = (P(None, "pty", "tx", None), P("pty", "tx", None), P(), P())
    out_specs = P(None, "pty", "tx", None)
    return jax.shard_map(
        functools.partial(on_device, mesh.shape["pty"], mesh.shape["tx"]),
        mesh=mesh, in_specs=in_specs, out_specs=out_specs, check_vma=False,
    )
```

```python
import functools

import jax
import jax.numpy as jnp
from jax import lax
from jax.experimental import pallas as pl
from jax.experimental.pallas import tpu as pltpu
from jax.sharding import PartitionSpec as P

STEP = 0.5
MESH = pl.DeviceIdType.MESH
ORDER = (0, 3, 1, 2, 4)
U, PR, V, W, B = range(5)
(SEND_UP, RECV_UP, SEND_DN, RECV_DN, SEND_L, RECV_L, SEND_R, RECV_R, ONE_C, ONE_C2, ONE_R,
 ONE_R2, TABLE, TWO, BACK_C, BACK_R, LOAD) = range(17)


def divide(x, d, limit):
    if d & (d - 1) == 0:
        return x >> (d.bit_length() - 1)
    factor = (1 << 16) // d + 1
    assert all((i * factor) >> 16 == i // d for i in range(limit)) and limit * factor < 2**31
    return (x * factor) >> 16


def kernel(n, t_count, rows, cols, levels, state, speed, freq, adj, out, buf, col, row, halo,
           tab, pick, back_c, back_r, junk, junk_r, junk2, speed_v, freq_v, work, sems):
    panel = cols * t_count
    total = 6 * panel
    shift = rows // 2
    row_blocks, col_blocks = rows // 4, cols // 4
    blocks = panel // 4
    groups = blocks // 2
    pairs = n // 4
    stride = max(1, t_count // -(-groups // pairs))
    edges = [(k * panel + shift) // rows for k in range(6)]
    places = [(k * panel + shift) % rows for k in range(6)]
    mask = sum(1 << m for m in range(n // 2) if 2 * m in edges)

    pty = lax.axis_index("pty")
    tx = lax.axis_index("tx")
    up = jnp.where(pty == 0, n - 1, pty - 1)
    down = jnp.where(pty == n - 1, 0, pty + 1)
    at_west = tx == 0
    at_east = tx == t_count - 1
    on_edge = at_west | at_east

    first_row = jnp.int32(-1)
    start_panel = jnp.int32(0)
    for k in range(6):
        first_row = jnp.where(pty == edges[k], places[k], first_row)
        start_panel = jnp.where(pty == edges[k], k, start_panel)
    has_start = first_row >= 0

    def holder(half, group):
        pair = group % pairs if pairs & (pairs - 1) else group & (pairs - 1)
        place = half * pairs + pair
        return (2 * place + ((mask >> place) & 1), divide(group, pairs, 4096) * stride)

    my_place = pty >> 1
    my_half = divide(my_place, pairs, 4096)
    my_pair = my_place - my_half * pairs
    my_group = divide(tx, stride, 4096) * pairs + my_pair
    is_holder = (
        ((pty & 1) == ((mask >> my_place) & 1))
        & (tx == divide(tx, stride, 4096) * stride)
        & (my_group < groups)
    )

    def push(src, dst, spare, send, recv, there):
        same = (there[0] == pty) & (there[1] == tx)

        @pl.when(same)
        def _():
            pltpu.make_async_copy(src, dst, recv).start()
            pltpu.make_async_copy(src, spare, send).start()

        @pl.when(jnp.logical_not(same))
        def _():
            pltpu.make_async_remote_copy(
                src_ref=src, dst_ref=dst, send_sem=send, recv_sem=recv,
                device_id=there, device_id_type=MESH,
            ).start()

    def done(ref, sem):
        pltpu.make_async_copy(ref, ref, sem).wait()

    barrier = pltpu.get_barrier_semaphore()
    for a in range(n):
        for c in range(t_count):
            if a == 0 and c == 0:
                continue
            there = pty + a
            there = jnp.where(there >= n, there - n, there)
            there_tx = tx + c
            there_tx = jnp.where(there_tx >= t_count, there_tx - t_count, there_tx)
            pl.semaphore_signal(barrier, inc=1, device_id=(there, there_tx), device_id_type=MESH)

    loads = [
        pltpu.make_async_copy(state.at[ORDER[f]], buf.at[0, f, pl.ds(1, rows)], sems.at[LOAD, 0])
        for f in range(5)
    ]
    for copy in loads:
        copy.start()
    load_speed = pltpu.make_async_copy(speed, speed_v, sems.at[LOAD, 1])
    load_speed.start()
    load_freq = pltpu.make_async_copy(freq, freq_v, sems.at[LOAD, 2])
    load_freq.start()
    done(buf.at[0, :, pl.ds(1, rows)], sems.at[LOAD, 0])

    lane = lax.broadcasted_iota(jnp.int32, (cols, levels), 1)
    line = lax.broadcasted_iota(jnp.int32, (cols, levels), 0)
    low, high = lane == 0, lane == levels - 1
    lev_half = jnp.where(low | high, 1.0, 0.5).astype(jnp.float32)
    west_line, east_line = line == 0, line == cols - 1
    col_half = jnp.where((west_line & at_west) | (east_line & at_east), 1.0, 0.5).astype(jnp.float32)
    sub = lax.broadcasted_iota(jnp.int32, (8, levels), 0)
    west_sign = jnp.where(at_west, -1.0, 1.0).astype(jnp.float32)

    def row_sends(s, there, src_row, dst_row, send, recv):
        return pltpu.make_async_remote_copy(
            src_ref=buf.at[s, pl.ds(0, 2), src_row], dst_ref=buf.at[s, pl.ds(0, 2), dst_row],
            send_sem=sems.at[send, s], recv_sem=sems.at[recv, s],
            device_id=(there, tx), device_id_type=MESH,
        )

    def col_sends(s, there, side, send, recv):
        return pltpu.make_async_remote_copy(
            src_ref=col.at[s, side], dst_ref=halo.at[s, 1 - side],
            send_sem=sems.at[send, s], recv_sem=sems.at[recv, s],
            device_id=(pty, there), device_id_type=MESH,
        )

    def stage(s, carry):
        weight_base = jnp.where(s == 0, 0.0, jnp.where(s == 1, 0.75, 1.0 / 3.0)).astype(jnp.float32)
        weight_new = jnp.where(s == 0, 1.0, jnp.where(s == 1, 0.25, 2.0 / 3.0)).astype(jnp.float32)
        weight_rate = weight_new * STEP

        def pack_col(ib, carry):
            for side in range(2):
                j = 0 if side == 0 else cols - 1
                for t in range(4):
                    i = 1 + 4 * ib + t
                    p = buf[s, PR, i, j : j + 1]
                    v = buf[s, V, i, j : j + 1]
                    col[s, side, ib, t : t + 1] = p
                    col[s, side, ib, 4 + t : 5 + t] = v * west_sign if side == 0 else v
            return carry

        lax.fori_loop(0, row_blocks, pack_col, 0)

        @pl.when(has_start)
        def _():
            for e in range(2):
                i = first_row + 1 - e
                for m in range(col_blocks // 2):
                    p = buf[s, PR, i, 8 * m : 8 * m + 8]
                    u = buf[s, U, i, 8 * m : 8 * m + 8]
                    if e == 0:
                        u = -u
                    row[s, e, 2 * m] = jnp.where(sub < 4, p, pltpu.roll(u, 4, 0))
                    row[s, e, 2 * m + 1] = jnp.where(sub < 4, pltpu.roll(p, 4, 0), u)

        @pl.when(s == 0)
        def _():
            pl.semaphore_wait(barrier, n * t_count - 1)
            load_freq.wait()

        @pl.when(on_edge)
        def _():
            side = jnp.where(at_west, 0, 1)

            def one(ib, carry):
                place = pty * rows + 4 * ib - shift
                place = jnp.where(place < 0, place + total, place)
                k = divide(place, panel, total)
                b = (place - k * panel) >> 2
                far = b >= groups
                slot = 24 + k * 4 + jnp.where(at_west, 2, 0) + jnp.where(far, 1, 0)
                group = jnp.where(far, blocks - 1 - b, b)
                for half in range(2):
                    push(col.at[s, side, ib], tab.at[s, slot], junk.at[s, half, ib],
                         sems.at[ONE_C + half, s], sems.at[TABLE, s], holder(half, group))
                return carry

            lax.fori_loop(0, row_blocks, one, 0)

        @pl.when(has_start)
        def _():
            def one(m, carry):
                b = tx * col_blocks + m
                far = b >= groups
                group = jnp.where(far, blocks - 1 - b, b)
                slot = (start_panel * 2 + jnp.where(far, 1, 0)) * 2
                for half in range(2):
                    push(row.at[s, :, m], tab.at[s, pl.ds(slot, 2)], junk_r.at[s, half, m],
                         sems.at[ONE_R + half, s], sems.at[TABLE, s], holder(half, group))
                return carry

            lax.fori_loop(0, col_blocks, one, 0)

        row_sends(s, up, 1, rows + 1, SEND_UP, RECV_UP).start()
        row_sends(s, down, rows, 0, SEND_DN, RECV_DN).start()

        @pl.when(tx > 0)
        def _():
            col_sends(s, tx - 1, 0, SEND_L, RECV_L).start()

        @pl.when(tx < t_count - 1)
        def _():
            col_sends(s, tx + 1, 1, SEND_R, RECV_R).start()

        def vertical(ib, carry):
            rate = weight_rate * freq_v[0:1]
            for t in range(4):
                i = 1 + 4 * ib + t
                p, w, b = buf[s, PR, i], buf[s, W, i], buf[s, B, i]
                above = jnp.where(high, p, pltpu.roll(p, levels - 1, 1))
                below = jnp.where(low, p, pltpu.roll(p, 1, 1))
                diff = lev_half * (above - below)
                buf[s + 1, W, i] = weight_base * buf[0, W, i] + (weight_new * w + weight_rate * (b - diff))
                buf[s + 1, B, i] = weight_base * buf[0, B, i] + (weight_new * b - rate * w)
            return carry

        lax.fori_loop(0, row_blocks, vertical, 0)

        @pl.when(is_holder)
        def _():
            done(tab.at[s], sems.at[TABLE, s])
            work[...] = tab[s]

            def one(kk, carry):
                k = my_half * 3 + kk
                before = jnp.where(k == 0, 5, k - 1)

                def choose(panel_here, edge, far):
                    entry = (panel_here * 4 + edge) * 3
                    other, face, flip = adj[entry], adj[entry + 1], adj[entry + 2]
                    side = flip if far == 0 else 1 - flip
                    bound = jnp.where(face == 2, jnp.where(other == 5, 0, other + 1), other)
                    index = jnp.where((face & 1) == 0, bound * 4 + side * 2 + (face >> 1),
                                      24 + other * 4 + (face >> 1) * 2 + side)
                    value = work[index]
                    two = jnp.where((sub & 2) == 0, pltpu.roll(value, 6, 0), pltpu.roll(value, 2, 0))
                    turned = jnp.where((sub & 1) == 0, pltpu.roll(two, 7, 0), pltpu.roll(two, 1, 0))
                    return jnp.where(flip == 1, turned, value)

                for far in range(2):
                    b = my_group if far == 0 else blocks - 1 - my_group
                    place = k * panel + shift
                    owner = divide(place, rows, total)
                    owner_tx = divide(b, col_blocks, total)
                    slot = (kk * 2 + far) * 2
                    pick[s, slot] = choose(k, 0, far)
                    pick[s, slot + 1] = choose(before, 2, far)
                    push(pick.at[s, pl.ds(slot, 2)], back_r.at[s, :, b - owner_tx * col_blocks],
                         junk2.at[s, pl.ds(slot, 2)], sems.at[TWO, s], sems.at[BACK_R, s],
                         (owner, owner_tx))
                    place = k * panel + 4 * b + shift
                    place = jnp.where(place >= total, place - total, place)
                    owner = divide(place, rows, total)
                    index = (place - owner * rows) >> 2
                    for e in (1, 3):
                        slot = 12 + kk * 4 + far * 2 + e // 2
                        pick[s, slot] = choose(k, e, far)
                        push(pick.at[s, slot], back_c.at[s, index], junk2.at[s, slot],
                             sems.at[TWO, s], sems.at[BACK_C, s],
                             (owner, t_count - 1 if e == 1 else 0))
                return carry

            lax.fori_loop(0, 3, one, 0)

        row_sends(s, up, 1, rows + 1, SEND_UP, RECV_UP).wait_recv()
        row_sends(s, down, rows, 0, SEND_DN, RECV_DN).wait_recv()

        @pl.when(tx > 0)
        def _():
            done(halo.at[s, 0], sems.at[RECV_R, s])

        @pl.when(tx < t_count - 1)
        def _():
            done(halo.at[s, 1], sems.at[RECV_L, s])

        @pl.when(s == 0)
        def _():
            load_speed.wait()

        def horizontal(ib, carry):
            for t in range(4):
                i = 1 + 4 * ib + t
                is_start, is_end = i - 1 == first_row, i == first_row
                row_half = jnp.where(is_start | is_end, 1.0, 0.5).astype(jnp.float32)
                u, p, v, w = buf[s, U, i], buf[s, PR, i], buf[s, V, i], buf[s, W, i]

                def along_rows(f, here):
                    after = jnp.where(is_end, here, buf[s, f, i + 1])
                    before = jnp.where(is_start, here, buf[s, f, i - 1])
                    return row_half * (after - before)

                def along_cols(here, offset):
                    left = halo[s, 0, ib, offset + t : offset + t + 1]
                    right = halo[s, 1, ib, offset + t : offset + t + 1]
                    left = jnp.where(at_west, here[0:1], left)
                    right = jnp.where(at_east, here[cols - 1 :], right)
                    after = jnp.where(east_line, right, pltpu.roll(here, cols - 1, 0))
                    before = jnp.where(west_line, left, pltpu.roll(here, 1, 0))
                    return col_half * (after - before)

                above = jnp.where(high, -w, pltpu.roll(w, levels - 1, 1))
                below = jnp.where(low, -w, pltpu.roll(w, 1, 1))
                wall = lev_half * (above - below)
                buf[s + 1, U, i] = weight_base * buf[0, U, i] + (
                    weight_new * u - weight_rate * along_rows(PR, p))
                buf[s + 1, V, i] = weight_base * buf[0, V, i] + (
                    weight_new * v - weight_rate * along_cols(p, 0))
                buf[s + 1, PR, i] = weight_base * buf[0, PR, i] + (
                    weight_new * p - (weight_rate * speed_v[i - 1]) * (
                        along_rows(U, u) + along_cols(v, 4) + wall))
            return carry

        lax.fori_loop(0, row_blocks, horizontal, 0)

        @pl.when(has_start)
        def _():
            done(back_r.at[s], sems.at[BACK_R, s])
            for e in range(2):
                i = first_row + 1 - e
                sign = -1.0 if e == 0 else 1.0
                for m in range(col_blocks // 2):
                    one, two = back_r[s, e, 2 * m], back_r[s, e, 2 * m + 1]
                    p_there = jnp.where(sub < 4, one, pltpu.roll(two, 4, 0))
                    n_there = jnp.where(sub < 4, pltpu.roll(one, 4, 0), two)
                    at = pl.ds(8 * m, 8)
                    n_here = sign * buf[s, U, i, at]
                    buf[s + 1, PR, i, at] += weight_rate * speed_v[i - 1, at] * (n_here + n_there)
                    buf[s + 1, U, i, at] += (sign * weight_rate) * (buf[s, PR, i, at] - p_there)

        for side in range(2):
            @pl.when(at_west if side == 0 else at_east)
            def _():
                done(back_c.at[s], sems.at[BACK_C, s])
                sign = -1.0 if side == 0 else 1.0
                j = 0 if side == 0 else cols - 1

                def one(ib, carry):
                    for t in range(4):
                        i = 1 + 4 * ib + t
                        p_here = col[s, side, ib, t : t + 1]
                        n_here = col[s, side, ib, 4 + t : 5 + t]
                        p_there = back_c[s, ib, t : t + 1]
                        n_there = back_c[s, ib, 4 + t : 5 + t]
                        buf[s + 1, PR, i, j : j + 1] += (
                            weight_rate * speed_v[i - 1, j : j + 1] * (n_here + n_there))
                        buf[s + 1, V, i, j : j + 1] += (sign * weight_rate) * (p_here - p_there)
                    return carry

                lax.fori_loop(0, row_blocks, one, 0)

        return carry

    @pl.when(at_west)
    def _():
        halo[:, 0] = jnp.zeros((3, row_blocks, 8, levels), jnp.float32)

    @pl.when(at_east)
    def _():
        halo[:, 1] = jnp.zeros((3, row_blocks, 8, levels), jnp.float32)

    lax.fori_loop(0, 3, stage, 0)

    stores = [
        pltpu.make_async_copy(buf.at[3, f, pl.ds(1, rows)], out.at[ORDER[f]], sems.at[LOAD, 2])
        for f in range(5)
    ]
    for copy in stores:
        copy.start()

    def finish(s, carry):
        row_sends(s, up, 1, rows + 1, SEND_UP, RECV_UP).wait_send()
        row_sends(s, down, rows, 0, SEND_DN, RECV_DN).wait_send()

        @pl.when(tx > 0)
        def _():
            done(col.at[s, 0], sems.at[SEND_L, s])

        @pl.when(tx < t_count - 1)
        def _():
            done(col.at[s, 1], sems.at[SEND_R, s])

        for half in range(2):
            @pl.when(on_edge)
            def _():
                done(col.at[s, 0], sems.at[ONE_C + half, s])

            @pl.when(has_start)
            def _():
                done(row.at[s], sems.at[ONE_R + half, s])

        @pl.when(is_holder)
        def _():
            done(pick.at[s], sems.at[TWO, s])

        return carry

    lax.fori_loop(0, 3, finish, 0)
    done(buf.at[3, :, pl.ds(1, rows)], sems.at[LOAD, 2])


def on_device(n, t_count, state, speed, freq, adjacency):
    _, rows, cols, levels = state.shape
    rb, cb = rows // 4, cols // 4
    f32 = jnp.float32
    return pl.pallas_call(
        functools.partial(kernel, n, t_count, rows, cols, levels),
        out_shape=jax.ShapeDtypeStruct(state.shape, f32),
        in_specs=[
            pl.BlockSpec(memory_space=pltpu.HBM),
            pl.BlockSpec(memory_space=pltpu.HBM),
            pl.BlockSpec(memory_space=pltpu.HBM),
            pl.BlockSpec(memory_space=pltpu.SMEM),
        ],
        out_specs=pl.BlockSpec(memory_space=pl.ANY),
        scratch_shapes=[
            pltpu.VMEM((4, 5, rows + 2, cols, levels), f32),
            pltpu.VMEM((3, 2, rb, 8, levels), f32),
            pltpu.VMEM((3, 2, cb, 8, levels), f32),
            pltpu.VMEM((3, 2, rb, 8, levels), f32),
            pltpu.VMEM((3, 48, 8, levels), f32),
            pltpu.VMEM((3, 24, 8, levels), f32),
            pltpu.VMEM((3, rb, 8, levels), f32),
            pltpu.VMEM((3, 2, cb, 8, levels), f32),
            pltpu.VMEM((3, 2, rb, 8, levels), f32),
            pltpu.VMEM((3, 2, cb, 2, 8, levels), f32),
            pltpu.VMEM((3, 24, 8, levels), f32),
            pltpu.VMEM((rows, cols, levels), f32),
            pltpu.VMEM((1, levels), f32),
            pltpu.VMEM((48, 8, levels), f32),
            pltpu.SemaphoreType.DMA((17, 3)),
        ],
        compiler_params=pltpu.CompilerParams(
            has_side_effects=True, collective_id=0, vmem_limit_bytes=62 * 1024 * 1024
        ),
    )(state, speed, freq.reshape(1, levels), adjacency.reshape(-1))


def solution(mesh):
    in_specs = (P(None, "pty", "tx", None), P("pty", "tx", None), P(), P())
    out_specs = P(None, "pty", "tx", None)
    return jax.shard_map(
        functools.partial(on_device, mesh.shape["pty"], mesh.shape["tx"]),
        mesh=mesh, in_specs=in_specs, out_specs=out_specs, check_vma=False,
    )
```

```python
import functools

import jax
import jax.numpy as jnp
from jax import lax
from jax.experimental import pallas as pl
from jax.experimental.pallas import tpu as pltpu
from jax.sharding import PartitionSpec as P

STEP = 0.5
MESH = pl.DeviceIdType.MESH
ORDER = (0, 3, 1, 2, 4)
U, PR, V, W, B = range(5)
(SEND_UP, RECV_UP, SEND_DN, RECV_DN, SEND_L, RECV_L, SEND_R, RECV_R, ONE_C, ONE_C2, ONE_R,
 ONE_R2, TABLE, TWO, BACK_C, BACK_R, LOAD) = range(17)


def divide(x, d, limit):
    if d & (d - 1) == 0:
        return x >> (d.bit_length() - 1)
    factor = (1 << 16) // d + 1
    assert all((i * factor) >> 16 == i // d for i in range(limit)) and limit * factor < 2**31
    return (x * factor) >> 16


def kernel(n, t_count, rows, cols, levels, state, speed, freq, adj, out, buf, col, row, halo,
           tab, pick, back_c, back_r, junk, junk_r, junk2, speed_v, freq_v, work, sems):
    panel = cols * t_count
    total = 6 * panel
    shift = rows // 2
    row_blocks, col_blocks = rows // 4, cols // 4
    blocks = panel // 4
    groups = blocks // 2
    pairs = n // 4
    stride = max(1, t_count // -(-groups // pairs))
    edges = [(k * panel + shift) // rows for k in range(6)]
    places = [(k * panel + shift) % rows for k in range(6)]
    mask = sum(1 << m for m in range(n // 2) if 2 * m in edges)

    pty = lax.axis_index("pty")
    tx = lax.axis_index("tx")
    up = jnp.where(pty == 0, n - 1, pty - 1)
    down = jnp.where(pty == n - 1, 0, pty + 1)
    at_west = tx == 0
    at_east = tx == t_count - 1
    on_edge = at_west | at_east

    first_row = jnp.int32(-1)
    start_panel = jnp.int32(0)
    for k in range(6):
        first_row = jnp.where(pty == edges[k], places[k], first_row)
        start_panel = jnp.where(pty == edges[k], k, start_panel)
    has_start = first_row >= 0

    first_pair = n // 8

    def holder(group):
        pair = group % pairs if pairs & (pairs - 1) else group & (pairs - 1)
        place = first_pair + pair
        return (2 * place + ((mask >> place) & 1), divide(group, pairs, 4096) * stride)

    my_place = pty >> 1
    my_pair = my_place - first_pair
    my_group = divide(tx, stride, 4096) * pairs + my_pair
    is_holder = (
        ((pty & 1) == ((mask >> my_place) & 1))
        & (tx == divide(tx, stride, 4096) * stride)
        & (my_pair >= 0)
        & (my_pair < pairs)
        & (my_group < groups)
    )

    def push(src, dst, spare, send, recv, there):
        same = (there[0] == pty) & (there[1] == tx)

        @pl.when(same)
        def _():
            pltpu.make_async_copy(src, dst, recv).start()
            pltpu.make_async_copy(src, spare, send).start()

        @pl.when(jnp.logical_not(same))
        def _():
            pltpu.make_async_remote_copy(
                src_ref=src, dst_ref=dst, send_sem=send, recv_sem=recv,
                device_id=there, device_id_type=MESH,
            ).start()

    def done(ref, sem):
        pltpu.make_async_copy(ref, ref, sem).wait()

    barrier = pltpu.get_barrier_semaphore()
    for a in range(n):
        for c in range(t_count):
            if a == 0 and c == 0:
                continue
            there = pty + a
            there = jnp.where(there >= n, there - n, there)
            there_tx = tx + c
            there_tx = jnp.where(there_tx >= t_count, there_tx - t_count, there_tx)
            pl.semaphore_signal(barrier, inc=1, device_id=(there, there_tx), device_id_type=MESH)

    loads = [
        pltpu.make_async_copy(state.at[ORDER[f]], buf.at[0, f, pl.ds(1, rows)], sems.at[LOAD, 0])
        for f in range(5)
    ]
    for copy in loads:
        copy.start()
    load_speed = pltpu.make_async_copy(speed, speed_v, sems.at[LOAD, 1])
    load_speed.start()
    load_freq = pltpu.make_async_copy(freq, freq_v, sems.at[LOAD, 2])
    load_freq.start()
    done(buf.at[0, :, pl.ds(1, rows)], sems.at[LOAD, 0])

    lane = lax.broadcasted_iota(jnp.int32, (cols, levels), 1)
    line = lax.broadcasted_iota(jnp.int32, (cols, levels), 0)
    low, high = lane == 0, lane == levels - 1
    lev_half = jnp.where(low | high, 1.0, 0.5).astype(jnp.float32)
    west_line, east_line = line == 0, line == cols - 1
    col_half = jnp.where((west_line & at_west) | (east_line & at_east), 1.0, 0.5).astype(jnp.float32)
    sub = lax.broadcasted_iota(jnp.int32, (8, levels), 0)
    west_sign = jnp.where(at_west, -1.0, 1.0).astype(jnp.float32)

    def row_sends(s, there, src_row, dst_row, send, recv):
        return pltpu.make_async_remote_copy(
            src_ref=buf.at[s, pl.ds(0, 2), src_row], dst_ref=buf.at[s, pl.ds(0, 2), dst_row],
            send_sem=sems.at[send, s], recv_sem=sems.at[recv, s],
            device_id=(there, tx), device_id_type=MESH,
        )

    def col_sends(s, there, side, send, recv):
        return pltpu.make_async_remote_copy(
            src_ref=col.at[s, side], dst_ref=halo.at[s, 1 - side],
            send_sem=sems.at[send, s], recv_sem=sems.at[recv, s],
            device_id=(pty, there), device_id_type=MESH,
        )

    def store(f):
        return pltpu.make_async_copy(
            buf.at[3, f, pl.ds(1, rows)], out.at[ORDER[f]], sems.at[LOAD, 2 if f < W else 0])

    def stage(s, carry):
        weight_base = jnp.where(s == 0, 0.0, jnp.where(s == 1, 0.75, 1.0 / 3.0)).astype(jnp.float32)
        weight_new = jnp.where(s == 0, 1.0, jnp.where(s == 1, 0.25, 2.0 / 3.0)).astype(jnp.float32)
        weight_rate = weight_new * STEP

        def pack_col(ib, carry):
            for side in range(2):
                j = 0 if side == 0 else cols - 1
                for t in range(4):
                    i = 1 + 4 * ib + t
                    p = buf[s, PR, i, j : j + 1]
                    v = buf[s, V, i, j : j + 1]
                    col[s, side, ib, t : t + 1] = p
                    col[s, side, ib, 4 + t : 5 + t] = v * west_sign if side == 0 else v
            return carry

        lax.fori_loop(0, row_blocks, pack_col, 0)

        @pl.when(has_start)
        def _():
            for e in range(2):
                i = first_row + 1 - e
                for m in range(col_blocks // 2):
                    p = buf[s, PR, i, 8 * m : 8 * m + 8]
                    u = buf[s, U, i, 8 * m : 8 * m + 8]
                    if e == 0:
                        u = -u
                    row[s, e, 2 * m] = jnp.where(sub < 4, p, pltpu.roll(u, 4, 0))
                    row[s, e, 2 * m + 1] = jnp.where(sub < 4, pltpu.roll(p, 4, 0), u)

        @pl.when(s == 0)
        def _():
            pl.semaphore_wait(barrier, n * t_count - 1)
            load_freq.wait()

        @pl.when(has_start)
        def _():
            def one(m, carry):
                b = tx * col_blocks + m
                far = b >= groups
                group = jnp.where(far, blocks - 1 - b, b)
                slot = (start_panel * 2 + jnp.where(far, 1, 0)) * 2
                for half in range(1):
                    push(row.at[s, :, m], tab.at[s, pl.ds(slot, 2)], junk_r.at[s, half, m],
                         sems.at[ONE_R + half, s], sems.at[TABLE, s], holder(group))
                return carry

            lax.fori_loop(0, col_blocks, one, 0)

        @pl.when(on_edge)
        def _():
            side = jnp.where(at_west, 0, 1)

            def one(ib, carry):
                place = pty * rows + 4 * ib - shift
                place = jnp.where(place < 0, place + total, place)
                k = divide(place, panel, total)
                b = (place - k * panel) >> 2
                far = b >= groups
                slot = 24 + k * 4 + jnp.where(at_west, 2, 0) + jnp.where(far, 1, 0)
                group = jnp.where(far, blocks - 1 - b, b)
                for half in range(1):
                    push(col.at[s, side, ib], tab.at[s, slot], junk.at[s, half, ib],
                         sems.at[ONE_C + half, s], sems.at[TABLE, s], holder(group))
                return carry

            lax.fori_loop(0, row_blocks, one, 0)

        row_sends(s, up, 1, rows + 1, SEND_UP, RECV_UP).start()
        row_sends(s, down, rows, 0, SEND_DN, RECV_DN).start()

        @pl.when(tx > 0)
        def _():
            col_sends(s, tx - 1, 0, SEND_L, RECV_L).start()

        @pl.when(tx < t_count - 1)
        def _():
            col_sends(s, tx + 1, 1, SEND_R, RECV_R).start()

        def vertical(ib, carry):
            rate = weight_rate * freq_v[0:1]
            for t in range(4):
                i = 1 + 4 * ib + t
                p, w, b = buf[s, PR, i], buf[s, W, i], buf[s, B, i]
                above = jnp.where(high, p, pltpu.roll(p, levels - 1, 1))
                below = jnp.where(low, p, pltpu.roll(p, 1, 1))
                diff = lev_half * (above - below)
                buf[s + 1, W, i] = weight_base * buf[0, W, i] + (weight_new * w + weight_rate * (b - diff))
                buf[s + 1, B, i] = weight_base * buf[0, B, i] + (weight_new * b - rate * w)
            return carry

        lax.fori_loop(0, row_blocks, vertical, 0)

        @pl.when(s == 2)
        def _():
            for f in (W, B):
                store(f).start()

        @pl.when(is_holder)
        def _():
            done(tab.at[s], sems.at[TABLE, s])
            work[...] = tab[s]

            def one(kk, carry):
                k = kk
                before = jnp.where(k == 0, 5, k - 1)

                def choose(panel_here, edge, far):
                    entry = (panel_here * 4 + edge) * 3
                    other, face, flip = adj[entry], adj[entry + 1], adj[entry + 2]
                    side = flip if far == 0 else 1 - flip
                    bound = jnp.where(face == 2, jnp.where(other == 5, 0, other + 1), other)
                    index = jnp.where((face & 1) == 0, bound * 4 + side * 2 + (face >> 1),
                                      24 + other * 4 + (face >> 1) * 2 + side)
                    value = work[index]
                    two = jnp.where((sub & 2) == 0, pltpu.roll(value, 6, 0), pltpu.roll(value, 2, 0))
                    turned = jnp.where((sub & 1) == 0, pltpu.roll(two, 7, 0), pltpu.roll(two, 1, 0))
                    return jnp.where(flip == 1, turned, value)

                for far in range(2):
                    b = my_group if far == 0 else blocks - 1 - my_group
                    place = k * panel + shift
                    owner = divide(place, rows, total)
                    owner_tx = divide(b, col_blocks, total)
                    slot = (kk * 2 + far) * 2
                    pick[s, slot] = choose(k, 0, far)
                    pick[s, slot + 1] = choose(before, 2, far)
                    push(pick.at[s, pl.ds(slot, 2)], back_r.at[s, :, b - owner_tx * col_blocks],
                         junk2.at[s, pl.ds(slot, 2)], sems.at[TWO, s], sems.at[BACK_R, s],
                         (owner, owner_tx))
                    place = k * panel + 4 * b + shift
                    place = jnp.where(place >= total, place - total, place)
                    owner = divide(place, rows, total)
                    index = (place - owner * rows) >> 2
                    for e in (1, 3):
                        slot = 24 + kk * 4 + far * 2 + e // 2
                        pick[s, slot] = choose(k, e, far)
                        push(pick.at[s, slot], back_c.at[s, index], junk2.at[s, slot],
                             sems.at[TWO, s], sems.at[BACK_C, s],
                             (owner, t_count - 1 if e == 1 else 0))
                return carry

            lax.fori_loop(0, 6, one, 0)

        row_sends(s, up, 1, rows + 1, SEND_UP, RECV_UP).wait_recv()
        row_sends(s, down, rows, 0, SEND_DN, RECV_DN).wait_recv()

        @pl.when(tx > 0)
        def _():
            done(halo.at[s, 0], sems.at[RECV_R, s])

        @pl.when(tx < t_count - 1)
        def _():
            done(halo.at[s, 1], sems.at[RECV_L, s])

        @pl.when(s == 0)
        def _():
            load_speed.wait()

        def horizontal(ib, carry):
            for t in range(4):
                i = 1 + 4 * ib + t
                is_start, is_end = i - 1 == first_row, i == first_row
                row_half = jnp.where(is_start | is_end, 1.0, 0.5).astype(jnp.float32)
                u, p, v, w = buf[s, U, i], buf[s, PR, i], buf[s, V, i], buf[s, W, i]

                def along_rows(f, here):
                    after = jnp.where(is_end, here, buf[s, f, i + 1])
                    before = jnp.where(is_start, here, buf[s, f, i - 1])
                    return row_half * (after - before)

                def along_cols(here, offset):
                    left = halo[s, 0, ib, offset + t : offset + t + 1]
                    right = halo[s, 1, ib, offset + t : offset + t + 1]
                    left = jnp.where(at_west, here[0:1], left)
                    right = jnp.where(at_east, here[cols - 1 :], right)
                    after = jnp.where(east_line, right, pltpu.roll(here, cols - 1, 0))
                    before = jnp.where(west_line, left, pltpu.roll(here, 1, 0))
                    return col_half * (after - before)

                above = jnp.where(high, -w, pltpu.roll(w, levels - 1, 1))
                below = jnp.where(low, -w, pltpu.roll(w, 1, 1))
                wall = lev_half * (above - below)
                buf[s + 1, U, i] = weight_base * buf[0, U, i] + (
                    weight_new * u - weight_rate * along_rows(PR, p))
                buf[s + 1, V, i] = weight_base * buf[0, V, i] + (
                    weight_new * v - weight_rate * along_cols(p, 0))
                buf[s + 1, PR, i] = weight_base * buf[0, PR, i] + (
                    weight_new * p - (weight_rate * speed_v[i - 1]) * (
                        along_rows(U, u) + along_cols(v, 4) + wall))
            return carry

        lax.fori_loop(0, row_blocks, horizontal, 0)

        @pl.when(has_start)
        def _():
            done(back_r.at[s], sems.at[BACK_R, s])
            for e in range(2):
                i = first_row + 1 - e
                sign = -1.0 if e == 0 else 1.0
                for m in range(col_blocks // 2):
                    one, two = back_r[s, e, 2 * m], back_r[s, e, 2 * m + 1]
                    p_there = jnp.where(sub < 4, one, pltpu.roll(two, 4, 0))
                    n_there = jnp.where(sub < 4, pltpu.roll(one, 4, 0), two)
                    at = pl.ds(8 * m, 8)
                    n_here = sign * buf[s, U, i, at]
                    buf[s + 1, PR, i, at] += weight_rate * speed_v[i - 1, at] * (n_here + n_there)
                    buf[s + 1, U, i, at] += (sign * weight_rate) * (buf[s, PR, i, at] - p_there)

        for side in range(2):
            @pl.when(at_west if side == 0 else at_east)
            def _():
                done(back_c.at[s], sems.at[BACK_C, s])
                sign = -1.0 if side == 0 else 1.0
                j = 0 if side == 0 else cols - 1

                def one(ib, carry):
                    for t in range(4):
                        i = 1 + 4 * ib + t
                        p_here = col[s, side, ib, t : t + 1]
                        n_here = col[s, side, ib, 4 + t : 5 + t]
                        p_there = back_c[s, ib, t : t + 1]
                        n_there = back_c[s, ib, 4 + t : 5 + t]
                        buf[s + 1, PR, i, j : j + 1] += (
                            weight_rate * speed_v[i - 1, j : j + 1] * (n_here + n_there))
                        buf[s + 1, V, i, j : j + 1] += (sign * weight_rate) * (p_here - p_there)
                    return carry

                lax.fori_loop(0, row_blocks, one, 0)

        return carry

    @pl.when(at_west)
    def _():
        halo[:, 0] = jnp.zeros((3, row_blocks, 8, levels), jnp.float32)

    @pl.when(at_east)
    def _():
        halo[:, 1] = jnp.zeros((3, row_blocks, 8, levels), jnp.float32)

    lax.fori_loop(0, 3, stage, 0)

    for f in (U, PR, V):
        store(f).start()

    def finish(s, carry):
        row_sends(s, up, 1, rows + 1, SEND_UP, RECV_UP).wait_send()
        row_sends(s, down, rows, 0, SEND_DN, RECV_DN).wait_send()

        @pl.when(tx > 0)
        def _():
            done(col.at[s, 0], sems.at[SEND_L, s])

        @pl.when(tx < t_count - 1)
        def _():
            done(col.at[s, 1], sems.at[SEND_R, s])

        for half in range(1):
            @pl.when(on_edge)
            def _():
                done(col.at[s, 0], sems.at[ONE_C + half, s])

            @pl.when(has_start)
            def _():
                done(row.at[s], sems.at[ONE_R + half, s])

        @pl.when(is_holder)
        def _():
            done(pick.at[s], sems.at[TWO, s])

        return carry

    lax.fori_loop(0, 3, finish, 0)
    done(buf.at[3, pl.ds(0, 3), pl.ds(1, rows)], sems.at[LOAD, 2])
    done(buf.at[3, pl.ds(3, 2), pl.ds(1, rows)], sems.at[LOAD, 0])


def on_device(n, t_count, state, speed, freq, adjacency):
    _, rows, cols, levels = state.shape
    rb, cb = rows // 4, cols // 4
    f32 = jnp.float32
    return pl.pallas_call(
        functools.partial(kernel, n, t_count, rows, cols, levels),
        out_shape=jax.ShapeDtypeStruct(state.shape, f32),
        in_specs=[
            pl.BlockSpec(memory_space=pltpu.HBM),
            pl.BlockSpec(memory_space=pltpu.HBM),
            pl.BlockSpec(memory_space=pltpu.HBM),
            pl.BlockSpec(memory_space=pltpu.SMEM),
        ],
        out_specs=pl.BlockSpec(memory_space=pl.ANY),
        scratch_shapes=[
            pltpu.VMEM((4, 5, rows + 2, cols, levels), f32),
            pltpu.VMEM((3, 2, rb, 8, levels), f32),
            pltpu.VMEM((3, 2, cb, 8, levels), f32),
            pltpu.VMEM((3, 2, rb, 8, levels), f32),
            pltpu.VMEM((3, 48, 8, levels), f32),
            pltpu.VMEM((3, 48, 8, levels), f32),
            pltpu.VMEM((3, rb, 8, levels), f32),
            pltpu.VMEM((3, 2, cb, 8, levels), f32),
            pltpu.VMEM((3, 2, rb, 8, levels), f32),
            pltpu.VMEM((3, 2, cb, 2, 8, levels), f32),
            pltpu.VMEM((3, 48, 8, levels), f32),
            pltpu.VMEM((rows, cols, levels), f32),
            pltpu.VMEM((1, levels), f32),
            pltpu.VMEM((48, 8, levels), f32),
            pltpu.SemaphoreType.DMA((17, 3)),
        ],
        compiler_params=pltpu.CompilerParams(
            has_side_effects=True, collective_id=0, vmem_limit_bytes=62 * 1024 * 1024
        ),
    )(state, speed, freq.reshape(1, levels), adjacency.reshape(-1))


def solution(mesh):
    in_specs = (P(None, "pty", "tx", None), P("pty", "tx", None), P(), P())
    out_specs = P(None, "pty", "tx", None)
    return jax.shard_map(
        functools.partial(on_device, mesh.shape["pty"], mesh.shape["tx"]),
        mesh=mesh, in_specs=in_specs, out_specs=out_specs, check_vma=False,
    )
```

```python
import functools

import jax
import jax.numpy as jnp
from jax import lax
from jax.experimental import pallas as pl
from jax.experimental.pallas import tpu as pltpu
from jax.sharding import PartitionSpec as P

STEP = 0.5
MESH = pl.DeviceIdType.MESH
ORDER = (0, 3, 1, 2, 4)
U, PR, V, W, B = range(5)
(SEND_UP, RECV_UP, SEND_DN, RECV_DN, SEND_L, RECV_L, SEND_R, RECV_R, ONE_C, ONE_C2, ONE_R,
 ONE_R2, TABLE, TWO, BACK_C, BACK_R, LOAD) = range(17)


def divide(x, d, limit):
    if d & (d - 1) == 0:
        return x >> (d.bit_length() - 1)
    factor = (1 << 16) // d + 1
    assert all((i * factor) >> 16 == i // d for i in range(limit)) and limit * factor < 2**31
    return (x * factor) >> 16


def kernel(n, t_count, rows, cols, levels, state, speed, freq, adj, out, buf, col, row, halo,
           tab, pick, back_c, back_r, junk, junk_r, junk2, speed_v, freq_v, work, sems):
    panel = cols * t_count
    total = 6 * panel
    shift = rows // 2
    row_blocks, col_blocks = rows // 4, cols // 4
    blocks = panel // 4
    groups = blocks // 2
    pairs = n // 4
    stride = max(1, t_count // -(-groups // pairs))
    edges = [(k * panel + shift) // rows for k in range(6)]
    places = [(k * panel + shift) % rows for k in range(6)]
    mask = sum(1 << m for m in range(n // 2) if 2 * m in edges)

    pty = lax.axis_index("pty")
    tx = lax.axis_index("tx")
    up = jnp.where(pty == 0, n - 1, pty - 1)
    down = jnp.where(pty == n - 1, 0, pty + 1)
    at_west = tx == 0
    at_east = tx == t_count - 1
    on_edge = at_west | at_east

    first_row = jnp.int32(-1)
    start_panel = jnp.int32(0)
    for k in range(6):
        first_row = jnp.where(pty == edges[k], places[k], first_row)
        start_panel = jnp.where(pty == edges[k], k, start_panel)
    has_start = first_row >= 0

    first_pair = n // 8

    def holder(group):
        pair = group % pairs if pairs & (pairs - 1) else group & (pairs - 1)
        place = first_pair + pair
        return (2 * place + ((mask >> place) & 1), divide(group, pairs, 4096) * stride)

    my_place = pty >> 1
    my_pair = my_place - first_pair
    my_group = divide(tx, stride, 4096) * pairs + my_pair
    is_holder = (
        ((pty & 1) == ((mask >> my_place) & 1))
        & (tx == divide(tx, stride, 4096) * stride)
        & (my_pair >= 0)
        & (my_pair < pairs)
        & (my_group < groups)
    )

    def push(src, dst, spare, send, recv, there):
        same = (there[0] == pty) & (there[1] == tx)

        @pl.when(same)
        def _():
            pltpu.make_async_copy(src, dst, recv).start()
            pltpu.make_async_copy(src, spare, send).start()

        @pl.when(jnp.logical_not(same))
        def _():
            pltpu.make_async_remote_copy(
                src_ref=src, dst_ref=dst, send_sem=send, recv_sem=recv,
                device_id=there, device_id_type=MESH,
            ).start()

    def done(ref, sem):
        pltpu.make_async_copy(ref, ref, sem).wait()

    barrier = pltpu.get_barrier_semaphore()
    for a in range(n):
        for c in range(t_count):
            if a == 0 and c == 0:
                continue
            there = pty + a
            there = jnp.where(there >= n, there - n, there)
            there_tx = tx + c
            there_tx = jnp.where(there_tx >= t_count, there_tx - t_count, there_tx)
            pl.semaphore_signal(barrier, inc=1, device_id=(there, there_tx), device_id_type=MESH)

    loads = [
        pltpu.make_async_copy(state.at[ORDER[f]], buf.at[0, f, pl.ds(1, rows)], sems.at[LOAD, 0])
        for f in range(5)
    ]
    for copy in loads:
        copy.start()
    load_speed = pltpu.make_async_copy(speed, speed_v, sems.at[LOAD, 1])
    load_speed.start()
    load_freq = pltpu.make_async_copy(freq, freq_v, sems.at[LOAD, 2])
    load_freq.start()
    done(buf.at[0, :, pl.ds(1, rows)], sems.at[LOAD, 0])

    lane = lax.broadcasted_iota(jnp.int32, (cols, levels), 1)
    line = lax.broadcasted_iota(jnp.int32, (cols, levels), 0)
    low, high = lane == 0, lane == levels - 1
    lev_half = jnp.where(low | high, 1.0, 0.5).astype(jnp.float32)
    west_line, east_line = line == 0, line == cols - 1
    col_half = jnp.where((west_line & at_west) | (east_line & at_east), 1.0, 0.5).astype(jnp.float32)
    sub = lax.broadcasted_iota(jnp.int32, (8, levels), 0)
    west_sign = jnp.where(at_west, -1.0, 1.0).astype(jnp.float32)

    def row_sends(s, there, src_row, dst_row, send, recv):
        return pltpu.make_async_remote_copy(
            src_ref=buf.at[s, pl.ds(0, 2), src_row], dst_ref=buf.at[s, pl.ds(0, 2), dst_row],
            send_sem=sems.at[send, s], recv_sem=sems.at[recv, s],
            device_id=(there, tx), device_id_type=MESH,
        )

    def col_sends(s, there, side, send, recv):
        return pltpu.make_async_remote_copy(
            src_ref=col.at[s, side], dst_ref=halo.at[s, 1 - side],
            send_sem=sems.at[send, s], recv_sem=sems.at[recv, s],
            device_id=(pty, there), device_id_type=MESH,
        )

    def store(f):
        return pltpu.make_async_copy(
            buf.at[3, f, pl.ds(1, rows)], out.at[ORDER[f]], sems.at[LOAD, 2 if f < W else 0])

    def stage(s, carry):
        weight_base = jnp.where(s == 0, 0.0, jnp.where(s == 1, 0.75, 1.0 / 3.0)).astype(jnp.float32)
        weight_new = jnp.where(s == 0, 1.0, jnp.where(s == 1, 0.25, 2.0 / 3.0)).astype(jnp.float32)
        weight_rate = weight_new * STEP

        def pack_col(ib, carry):
            for side in range(2):
                j = 0 if side == 0 else cols - 1
                for t in range(4):
                    i = 1 + 4 * ib + t
                    p = buf[s, PR, i, j : j + 1]
                    v = buf[s, V, i, j : j + 1]
                    col[s, side, ib, t : t + 1] = p
                    col[s, side, ib, 4 + t : 5 + t] = v * west_sign if side == 0 else v
            return carry


        @pl.when(has_start)
        def _():
            for e in range(2):
                i = first_row + 1 - e
                for m in range(col_blocks // 2):
                    p = buf[s, PR, i, 8 * m : 8 * m + 8]
                    u = buf[s, U, i, 8 * m : 8 * m + 8]
                    if e == 0:
                        u = -u
                    row[s, e, 2 * m] = jnp.where(sub < 4, p, pltpu.roll(u, 4, 0))
                    row[s, e, 2 * m + 1] = jnp.where(sub < 4, pltpu.roll(p, 4, 0), u)

        @pl.when(s == 0)
        def _():
            pl.semaphore_wait(barrier, n * t_count - 1)
            load_freq.wait()

        @pl.when(has_start)
        def _():
            def one(m, carry):
                b = tx * col_blocks + m
                far = b >= groups
                group = jnp.where(far, blocks - 1 - b, b)
                slot = (start_panel * 2 + jnp.where(far, 1, 0)) * 2
                for half in range(1):
                    push(row.at[s, :, m], tab.at[s, pl.ds(slot, 2)], junk_r.at[s, half, m],
                         sems.at[ONE_R + half, s], sems.at[TABLE, s], holder(group))
                return carry

            lax.fori_loop(0, col_blocks, one, 0)

        lax.fori_loop(0, row_blocks, pack_col, 0)

        @pl.when(on_edge)
        def _():
            side = jnp.where(at_west, 0, 1)

            def one(ib, carry):
                place = pty * rows + 4 * ib - shift
                place = jnp.where(place < 0, place + total, place)
                k = divide(place, panel, total)
                b = (place - k * panel) >> 2
                far = b >= groups
                slot = 24 + k * 4 + jnp.where(at_west, 2, 0) + jnp.where(far, 1, 0)
                group = jnp.where(far, blocks - 1 - b, b)
                for half in range(1):
                    push(col.at[s, side, ib], tab.at[s, slot], junk.at[s, half, ib],
                         sems.at[ONE_C + half, s], sems.at[TABLE, s], holder(group))
                return carry

            lax.fori_loop(0, row_blocks, one, 0)

        row_sends(s, up, 1, rows + 1, SEND_UP, RECV_UP).start()
        row_sends(s, down, rows, 0, SEND_DN, RECV_DN).start()

        @pl.when(tx > 0)
        def _():
            col_sends(s, tx - 1, 0, SEND_L, RECV_L).start()

        @pl.when(tx < t_count - 1)
        def _():
            col_sends(s, tx + 1, 1, SEND_R, RECV_R).start()

        def vertical(ib, carry):
            rate = weight_rate * freq_v[0:1]
            for t in range(4):
                i = 1 + 4 * ib + t
                p, w, b = buf[s, PR, i], buf[s, W, i], buf[s, B, i]
                above = jnp.where(high, p, pltpu.roll(p, levels - 1, 1))
                below = jnp.where(low, p, pltpu.roll(p, 1, 1))
                diff = lev_half * (above - below)
                buf[s + 1, W, i] = weight_base * buf[0, W, i] + (weight_new * w + weight_rate * (b - diff))
                buf[s + 1, B, i] = weight_base * buf[0, B, i] + (weight_new * b - rate * w)
            return carry

        lax.fori_loop(0, row_blocks, vertical, 0)

        @pl.when(s == 2)
        def _():
            for f in (W, B):
                store(f).start()

        @pl.when(is_holder)
        def _():
            done(tab.at[s], sems.at[TABLE, s])
            work[...] = tab[s]

            def one(kk, carry):
                k = kk
                before = jnp.where(k == 0, 5, k - 1)

                def choose(panel_here, edge, far):
                    entry = (panel_here * 4 + edge) * 3
                    other, face, flip = adj[entry], adj[entry + 1], adj[entry + 2]
                    side = flip if far == 0 else 1 - flip
                    bound = jnp.where(face == 2, jnp.where(other == 5, 0, other + 1), other)
                    index = jnp.where((face & 1) == 0, bound * 4 + side * 2 + (face >> 1),
                                      24 + other * 4 + (face >> 1) * 2 + side)
                    value = work[index]
                    two = jnp.where((sub & 2) == 0, pltpu.roll(value, 6, 0), pltpu.roll(value, 2, 0))
                    turned = jnp.where((sub & 1) == 0, pltpu.roll(two, 7, 0), pltpu.roll(two, 1, 0))
                    return jnp.where(flip == 1, turned, value)

                for far in range(2):
                    b = my_group if far == 0 else blocks - 1 - my_group
                    place = k * panel + shift
                    owner = divide(place, rows, total)
                    owner_tx = divide(b, col_blocks, total)
                    slot = (kk * 2 + far) * 2
                    pick[s, slot] = choose(k, 0, far)
                    pick[s, slot + 1] = choose(before, 2, far)
                    push(pick.at[s, pl.ds(slot, 2)], back_r.at[s, :, b - owner_tx * col_blocks],
                         junk2.at[s, pl.ds(slot, 2)], sems.at[TWO, s], sems.at[BACK_R, s],
                         (owner, owner_tx))
                    place = k * panel + 4 * b + shift
                    place = jnp.where(place >= total, place - total, place)
                    owner = divide(place, rows, total)
                    index = (place - owner * rows) >> 2
                    for e in (1, 3):
                        slot = 24 + kk * 4 + far * 2 + e // 2
                        pick[s, slot] = choose(k, e, far)
                        push(pick.at[s, slot], back_c.at[s, index], junk2.at[s, slot],
                             sems.at[TWO, s], sems.at[BACK_C, s],
                             (owner, t_count - 1 if e == 1 else 0))
                return carry

            lax.fori_loop(0, 6, one, 0)

        row_sends(s, up, 1, rows + 1, SEND_UP, RECV_UP).wait_recv()
        row_sends(s, down, rows, 0, SEND_DN, RECV_DN).wait_recv()

        @pl.when(tx > 0)
        def _():
            done(halo.at[s, 0], sems.at[RECV_R, s])

        @pl.when(tx < t_count - 1)
        def _():
            done(halo.at[s, 1], sems.at[RECV_L, s])

        @pl.when(s == 0)
        def _():
            load_speed.wait()

        def horizontal(ib, carry):
            for t in range(4):
                i = 1 + 4 * ib + t
                is_start, is_end = i - 1 == first_row, i == first_row
                row_half = jnp.where(is_start | is_end, 1.0, 0.5).astype(jnp.float32)
                u, p, v, w = buf[s, U, i], buf[s, PR, i], buf[s, V, i], buf[s, W, i]

                def along_rows(f, here):
                    after = jnp.where(is_end, here, buf[s, f, i + 1])
                    before = jnp.where(is_start, here, buf[s, f, i - 1])
                    return row_half * (after - before)

                def along_cols(here, offset):
                    left = halo[s, 0, ib, offset + t : offset + t + 1]
                    right = halo[s, 1, ib, offset + t : offset + t + 1]
                    left = jnp.where(at_west, here[0:1], left)
                    right = jnp.where(at_east, here[cols - 1 :], right)
                    after = jnp.where(east_line, right, pltpu.roll(here, cols - 1, 0))
                    before = jnp.where(west_line, left, pltpu.roll(here, 1, 0))
                    return col_half * (after - before)

                above = jnp.where(high, -w, pltpu.roll(w, levels - 1, 1))
                below = jnp.where(low, -w, pltpu.roll(w, 1, 1))
                wall = lev_half * (above - below)
                buf[s + 1, U, i] = weight_base * buf[0, U, i] + (
                    weight_new * u - weight_rate * along_rows(PR, p))
                buf[s + 1, V, i] = weight_base * buf[0, V, i] + (
                    weight_new * v - weight_rate * along_cols(p, 0))
                buf[s + 1, PR, i] = weight_base * buf[0, PR, i] + (
                    weight_new * p - (weight_rate * speed_v[i - 1]) * (
                        along_rows(U, u) + along_cols(v, 4) + wall))
            return carry

        lax.fori_loop(0, row_blocks, horizontal, 0)

        @pl.when(has_start)
        def _():
            done(back_r.at[s], sems.at[BACK_R, s])
            for e in range(2):
                i = first_row + 1 - e
                sign = -1.0 if e == 0 else 1.0
                for m in range(col_blocks // 2):
                    one, two = back_r[s, e, 2 * m], back_r[s, e, 2 * m + 1]
                    p_there = jnp.where(sub < 4, one, pltpu.roll(two, 4, 0))
                    n_there = jnp.where(sub < 4, pltpu.roll(one, 4, 0), two)
                    at = pl.ds(8 * m, 8)
                    n_here = sign * buf[s, U, i, at]
                    buf[s + 1, PR, i, at] += weight_rate * speed_v[i - 1, at] * (n_here + n_there)
                    buf[s + 1, U, i, at] += (sign * weight_rate) * (buf[s, PR, i, at] - p_there)

        for side in range(2):
            @pl.when(at_west if side == 0 else at_east)
            def _():
                done(back_c.at[s], sems.at[BACK_C, s])
                sign = -1.0 if side == 0 else 1.0
                j = 0 if side == 0 else cols - 1

                def one(ib, carry):
                    for t in range(4):
                        i = 1 + 4 * ib + t
                        p_here = col[s, side, ib, t : t + 1]
                        n_here = col[s, side, ib, 4 + t : 5 + t]
                        p_there = back_c[s, ib, t : t + 1]
                        n_there = back_c[s, ib, 4 + t : 5 + t]
                        buf[s + 1, PR, i, j : j + 1] += (
                            weight_rate * speed_v[i - 1, j : j + 1] * (n_here + n_there))
                        buf[s + 1, V, i, j : j + 1] += (sign * weight_rate) * (p_here - p_there)
                    return carry

                lax.fori_loop(0, row_blocks, one, 0)

        return carry

    @pl.when(at_west)
    def _():
        halo[:, 0] = jnp.zeros((3, row_blocks, 8, levels), jnp.float32)

    @pl.when(at_east)
    def _():
        halo[:, 1] = jnp.zeros((3, row_blocks, 8, levels), jnp.float32)

    lax.fori_loop(0, 3, stage, 0)

    for f in (U, PR, V):
        store(f).start()

    def finish(s, carry):
        row_sends(s, up, 1, rows + 1, SEND_UP, RECV_UP).wait_send()
        row_sends(s, down, rows, 0, SEND_DN, RECV_DN).wait_send()

        @pl.when(tx > 0)
        def _():
            done(col.at[s, 0], sems.at[SEND_L, s])

        @pl.when(tx < t_count - 1)
        def _():
            done(col.at[s, 1], sems.at[SEND_R, s])

        for half in range(1):
            @pl.when(on_edge)
            def _():
                done(col.at[s, 0], sems.at[ONE_C + half, s])

            @pl.when(has_start)
            def _():
                done(row.at[s], sems.at[ONE_R + half, s])

        @pl.when(is_holder)
        def _():
            done(pick.at[s], sems.at[TWO, s])

        return carry

    lax.fori_loop(0, 3, finish, 0)
    done(buf.at[3, pl.ds(0, 3), pl.ds(1, rows)], sems.at[LOAD, 2])
    done(buf.at[3, pl.ds(3, 2), pl.ds(1, rows)], sems.at[LOAD, 0])


def on_device(n, t_count, state, speed, freq, adjacency):
    _, rows, cols, levels = state.shape
    rb, cb = rows // 4, cols // 4
    f32 = jnp.float32
    return pl.pallas_call(
        functools.partial(kernel, n, t_count, rows, cols, levels),
        out_shape=jax.ShapeDtypeStruct(state.shape, f32),
        in_specs=[
            pl.BlockSpec(memory_space=pltpu.HBM),
            pl.BlockSpec(memory_space=pltpu.HBM),
            pl.BlockSpec(memory_space=pltpu.HBM),
            pl.BlockSpec(memory_space=pltpu.SMEM),
        ],
        out_specs=pl.BlockSpec(memory_space=pl.ANY),
        scratch_shapes=[
            pltpu.VMEM((4, 5, rows + 2, cols, levels), f32),
            pltpu.VMEM((3, 2, rb, 8, levels), f32),
            pltpu.VMEM((3, 2, cb, 8, levels), f32),
            pltpu.VMEM((3, 2, rb, 8, levels), f32),
            pltpu.VMEM((3, 48, 8, levels), f32),
            pltpu.VMEM((3, 48, 8, levels), f32),
            pltpu.VMEM((3, rb, 8, levels), f32),
            pltpu.VMEM((3, 2, cb, 8, levels), f32),
            pltpu.VMEM((3, 2, rb, 8, levels), f32),
            pltpu.VMEM((3, 2, cb, 2, 8, levels), f32),
            pltpu.VMEM((3, 48, 8, levels), f32),
            pltpu.VMEM((rows, cols, levels), f32),
            pltpu.VMEM((1, levels), f32),
            pltpu.VMEM((48, 8, levels), f32),
            pltpu.SemaphoreType.DMA((17, 3)),
        ],
        compiler_params=pltpu.CompilerParams(
            has_side_effects=True, collective_id=0, vmem_limit_bytes=62 * 1024 * 1024
        ),
    )(state, speed, freq.reshape(1, levels), adjacency.reshape(-1))


def solution(mesh):
    in_specs = (P(None, "pty", "tx", None), P("pty", "tx", None), P(), P())
    out_specs = P(None, "pty", "tx", None)
    return jax.shard_map(
        functools.partial(on_device, mesh.shape["pty"], mesh.shape["tx"]),
        mesh=mesh, in_specs=in_specs, out_specs=out_specs, check_vma=False,
    )
```
